32 devices in a mesh: section: 4 (over y, x), fsdp: 8 (over z, core).
Axes of the slice: x: 2, y: 2, z: 4, core: 2. Of those that a mesh axis runs over, the one named last changes fastest.
Arguments:
- residual_input: bfloat16 [2, 512, 8192], P(None, 'fsdp'), may hold values from -6 to 6
- output_gradient: bfloat16 [2, 512, 8192], P(None, 'fsdp'), may hold values from -0.01953125 to 0.01953125
- value_projection_weight: bfloat16 [4, 8192, 512], P('section', 'fsdp'), may hold values from -0.0625 to 0.0625
- output_weight: bfloat16 [4, 512, 8192], P('section', None, 'fsdp'), may hold values from -0.25 to 0.25
- adapter_down_weight: bfloat16 [4, 8192, 160], P('section'), may hold values from -0.0625 to 0.0625
- adapter_up_weight: bfloat16 [4, 160, 512], P('section'), may hold values from -0.625 to 0.625
- input_norm_scale: float32 [4, 8192], P('section'), may hold values from 0.25 to 1.75
- segment_adapter_index: int32 [2, 16], P(None, 'fsdp'), may hold values from 0 to 3
- adapter_rank_blocks: int32 [4], replicated, may hold values from 1 to 16, 20 in all
Outputs:
- grad_down: float32 [4, 8192, 160], P('section', 'fsdp')
- grad_up: float32 [4, 160, 512], P('section', None, 'fsdp')
The draws below stay inside these ranges and needn't reach their ends.
Inputs may be any that keep to these rules, and one draw needn't show every extreme that they name: `segment_adapter_index`: adapter of each block of 32 consecutive tokens. `adapter_rank_blocks`: the entries sum to 20.
All inputs are finite; a program needn't handle non-finite values.
Results may differ from the reference program's by a relative error of at most 0.014.
Values may be sent and summed in bfloat16 or wider, within the bound.
A program may use at most 128 MiB of HBM per device.

```python
import math
import jax
import jax.numpy as jnp
import numpy as np
from jax import lax

MODEL_WIDTH = 8192
VALUE_WIDTH = 512
ADAPTERS = 4
RMAX = 128
RBLOCKS = 20
SEG = 32
M = 2
LAYER_SECTIONS = 4
TOKENS = 512
PACKED_COLUMNS = 160


def set_ends(result, stream_key, smallest, largest):
    extent = result.shape
    spot = [jax.random.randint(jax.random.fold_in(stream_key, axis), (), 0, extent[axis]) for axis in range(len(extent))]
    result = result.at[tuple(spot)].set(smallest)
    longest = extent.index(max(extent))
    spot[longest] = (spot[longest] + 1) % extent[longest]
    return result.at[tuple(spot)].set(largest)


def spiked(array, rng, source, target, blocks, factor):
    owner, partner = [(jnp.arange(array.shape[position]) // (array.shape[position] // blocks)).reshape([-1 if axis == position else 1 for axis in range(array.ndim)]) for position in (source, target)]
    chosen = jax.random.permutation(rng, blocks)[partner]
    strong = (owner == chosen) | (owner == (partner + blocks // 2) % blocks)
    return jnp.where(strong, factor * array, array)


def block_scale(key, extent, split, low, top_value):
    def one(axis_at, shards_of):
        draws = jax.random.uniform(jax.random.fold_in(jax.random.fold_in(key, 6), axis_at), (shards_of,), jnp.float32, low / len(split), top_value / len(split))
        return jnp.repeat(jnp.exp(draws), extent[axis_at] // shards_of).reshape((-1,) + (1,) * (len(extent) - axis_at - 1))

    factor_of = one(*split[0])
    for cut in split[1:]:
        factor_of = factor_of * one(*cut)
    return factor_of


def length_profile(count, total, bound, lean):
    portions = [(1 << 20) // math.isqrt(standing ** lean) + 1 for standing in range(2, count + 1)]
    rest, given = total - bound - (count - 1), [1] * (count - 1)
    while rest > 0:
        candidates = [i for i in range(count - 1) if given[i] < bound]
        mass, budget = sum([portions[i] for i in candidates]), rest
        for i in candidates:
            addition = min(bound - given[i], max(1, budget * portions[i] // mass), rest)
            given[i] = given[i] + addition
            rest = rest - addition
    return np.array([bound] + given)


def uneven(own_key, number_of, total, limit, slope):
    if number_of == 2:
        one = jax.random.randint(own_key, (), max(1, total - limit), min(limit, total - 1) + 1)
        return jnp.stack([one, total - one])
    sizes = jnp.asarray(length_profile(number_of, total, limit, slope), jnp.int32)
    couples = (number_of - 1) // 2
    source_of, taker = sizes[1:1 + 2 * couples:2], sizes[2:2 + 2 * couples:2]
    margin = jnp.minimum(source_of - 1, limit - taker)
    moved = jax.random.randint(jax.random.fold_in(own_key, 1), (couples,), 0, 1 << 20) % (margin + 1)
    sizes = sizes.at[1:1 + 2 * couples:2].set(source_of - moved).at[2:2 + 2 * couples:2].set(taker + moved)
    return sizes[jax.random.permutation(jax.random.fold_in(own_key, 2), number_of)]


def noise(stream_key, shape, scale, bound, pieces=(), kind=jnp.bfloat16):
    values = jax.random.normal(stream_key, shape, jnp.float32) * scale
    if len(pieces) > 0:
        values = block_scale(stream_key, shape, pieces, -0.22, 0.18) * values
    return jnp.clip(values, min=-bound, max=bound).astype(kind)


def bell_draw_with(stream_key, dims, spread, bound, split, heavy, held_as=jnp.bfloat16):
    array = spread * jax.random.normal(stream_key, dims, jnp.float32)
    if split:
        array = array * block_scale(stream_key, dims, split, -0.22, 0.18)
    return jnp.clip(spiked(array, jax.random.fold_in(stream_key, 3), *heavy), -bound, bound).astype(held_as)


def setup_inputs(seed: int = 0) -> dict:
    keys = jax.random.split(jax.random.key(seed), 10)
    residual_input = bell_draw_with(keys[0], (M, TOKENS, MODEL_WIDTH), 1.0, 6.0, ((1, 8),), (1, 2, 8, 2.0))
    output_gradient = noise(keys[1], (M, TOKENS, MODEL_WIDTH), (0.1 / (M * TOKENS) ** 0.5), 0.01953125, ((1, 8),))
    value_projection_weight = noise(keys[2], (LAYER_SECTIONS, MODEL_WIDTH, VALUE_WIDTH), MODEL_WIDTH ** -0.5, 0.0625, ((0, 4), (1, 8)))
    output_weight = noise(keys[3], (LAYER_SECTIONS, VALUE_WIDTH, MODEL_WIDTH), VALUE_WIDTH ** -0.5, 0.25, ((0, 4), (2, 8)))
    adapter_down_weight = noise(keys[4], (LAYER_SECTIONS, MODEL_WIDTH, PACKED_COLUMNS), MODEL_WIDTH ** -0.5, 0.0625, ((0, 4),))
    adapter_up_weight = noise(keys[5], (LAYER_SECTIONS, PACKED_COLUMNS, VALUE_WIDTH), 0.1, 0.625, ((0, 4),))
    input_norm_scale = jnp.clip(1.0 + 0.15 * jax.random.normal(keys[6], (LAYER_SECTIONS, MODEL_WIDTH), jnp.float32), 0.25, 1.75)
    segment_adapter_index = set_ends(jax.random.randint(keys[7], (M, TOKENS // SEG), 0, ADAPTERS), jax.random.fold_in(keys[7], 1), 0, ADAPTERS - 1).astype(jnp.int32)
    adapter_rank_blocks = uneven(keys[8], ADAPTERS, RBLOCKS, RMAX // 8, 2).astype(jnp.int32)
    return {"residual_input": residual_input, "output_gradient": output_gradient, "value_projection_weight": value_projection_weight, "output_weight": output_weight, "adapter_down_weight": adapter_down_weight, "adapter_up_weight": adapter_up_weight, "input_norm_scale": input_norm_scale, "segment_adapter_index": segment_adapter_index, "adapter_rank_blocks": adapter_rank_blocks}


EPSILON = 1e-06
ADAPTER_ALPHA = 32.0

def coefficients(segments, adapter_rank_blocks):
    rank_sizes = 8 * adapter_rank_blocks
    rank_ends = jnp.cumsum(rank_sizes).astype(jnp.int32)
    columns = jnp.arange(PACKED_COLUMNS, dtype=jnp.int32)
    column_owner = lax.optimization_barrier(jnp.sum((columns[:, None] >= rank_ends[None, :]).astype(jnp.int32), axis=1))
    token_adapter = jnp.repeat(segments, SEG)
    selector = (token_adapter[:, None] == jnp.arange(ADAPTERS, dtype=jnp.int32)[None, :]).astype(jnp.float32)
    token_rank_mask = lax.optimization_barrier(jnp.sum(selector * rank_sizes.astype(jnp.float32)[None, :], axis=1))
    adapter_matches = (token_adapter[:, None] == column_owner[None, :]).astype(jnp.float32)
    return adapter_matches * (ADAPTER_ALPHA / token_rank_mask)[:, None]

def section_forward_pass(layer_activation, norm_gains, value_weight, out_weight, down_matrix, up_matrix, scale_coefficient):
    widened = layer_activation.astype(jnp.float32)
    inverse_root_mean = lax.rsqrt(lax.optimization_barrier(jnp.mean(widened * widened, axis=-1)) + EPSILON)
    normalized_input = (widened * inverse_root_mean[:, None] * norm_gains[None, :]).astype(jnp.bfloat16)
    rank_projection = (jnp.dot(normalized_input, down_matrix, preferred_element_type=jnp.float32) * scale_coefficient).astype(jnp.bfloat16)
    value = (jnp.dot(normalized_input, value_weight, preferred_element_type=jnp.float32) + jnp.dot(rank_projection, up_matrix, preferred_element_type=jnp.float32)).astype(jnp.bfloat16)
    section_output = (widened + jnp.dot(value, out_weight, preferred_element_type=jnp.float32)).astype(jnp.bfloat16)
    return (section_output, normalized_input, rank_projection, inverse_root_mean)

def contract(left, right, left_dim, right_dim):
    return lax.dot_general(left, right, (((left_dim,), (right_dim,)), ((), ())), preferred_element_type=jnp.float32)

def section_backward_pass(layer_activation, incoming_gradient, norm_gains, value_weight, out_weight, down_matrix, up_matrix, scale_coefficient, normalized_input, rank_projection, inverse_root_mean):
    value_grad = contract(incoming_gradient, out_weight, 1, 1).astype(jnp.bfloat16)
    up_product = contract(rank_projection, value_grad, 0, 0)
    low_grad = (contract(value_grad, up_matrix, 1, 1) * scale_coefficient).astype(jnp.bfloat16)
    down_product = contract(normalized_input, low_grad, 0, 0)
    normed_grad = contract(value_grad, value_weight, 1, 1) + contract(low_grad, down_matrix, 1, 1)
    widened = layer_activation.astype(jnp.float32)
    scaled = normed_grad * norm_gains[None, :]
    cubed = inverse_root_mean * inverse_root_mean * inverse_root_mean
    input_grad = incoming_gradient.astype(jnp.float32) + inverse_root_mean[:, None] * scaled - widened * cubed[:, None] * lax.optimization_barrier(jnp.mean(widened * scaled, axis=-1, keepdims=True))
    return (input_grad.astype(jnp.bfloat16), down_product, up_product)

def reference(residual_input, output_gradient, value_projection_weight, output_weight, adapter_down_weight, adapter_up_weight, input_norm_scale, segment_adapter_index, adapter_rank_blocks):
    down_sums = [jnp.zeros((MODEL_WIDTH, PACKED_COLUMNS), jnp.float32) for layer_position in range(LAYER_SECTIONS)]
    up_sums = [jnp.zeros((PACKED_COLUMNS, VALUE_WIDTH), jnp.float32) for layer_position in range(LAYER_SECTIONS)]
    for micro_index in range(M):
        scale_coefficient = coefficients(segment_adapter_index[micro_index], adapter_rank_blocks)
        layer_activation = residual_input[micro_index]
        saved = []
        for layer_position in range(LAYER_SECTIONS):
            section_output, normalized_input, rank_projection, inverse_root_mean = section_forward_pass(layer_activation, input_norm_scale[layer_position], value_projection_weight[layer_position], output_weight[layer_position], adapter_down_weight[layer_position], adapter_up_weight[layer_position], scale_coefficient)
            saved.append((layer_activation, normalized_input, rank_projection, inverse_root_mean))
            layer_activation = section_output
        incoming_gradient = output_gradient[micro_index]
        for layer_position in reversed(range(LAYER_SECTIONS)):
            layer_activation, normalized_input, rank_projection, inverse_root_mean = saved[layer_position]
            incoming_gradient, down_product, up_product = section_backward_pass(layer_activation, incoming_gradient, input_norm_scale[layer_position], value_projection_weight[layer_position], output_weight[layer_position], adapter_down_weight[layer_position], adapter_up_weight[layer_position], scale_coefficient, normalized_input, rank_projection, inverse_root_mean)
            down_sums[layer_position] = down_sums[layer_position] + down_product
            up_sums[layer_position] = up_sums[layer_position] + up_product
    return (jnp.stack(down_sums), jnp.stack(up_sums))
```

```python
import functools

import jax
import jax.numpy as jnp
from jax import lax
from jax.experimental import pallas as pl
from jax.experimental.pallas import tpu as pltpu
from jax.sharding import PartitionSpec as P

SEG = 32
EPSILON = 1e-06
ADAPTER_ALPHA = 32.0
LANES = 128
MESH = pl.DeviceIdType.MESH
F32 = jnp.float32
BF16 = jnp.bfloat16


def coefficients(segments, adapter_rank_blocks, columns_padded):
    adapters = adapter_rank_blocks.shape[0]
    rank_sizes = 8 * adapter_rank_blocks
    rank_ends = jnp.cumsum(rank_sizes)
    columns = jnp.arange(columns_padded, dtype=jnp.int32)
    column_owner = jnp.sum((columns[:, None] >= rank_ends[None, :]).astype(jnp.int32), axis=1)
    token_adapter = jnp.repeat(segments, SEG)
    selector = (token_adapter[:, None] == jnp.arange(adapters, dtype=jnp.int32)[None, :]).astype(F32)
    token_rank = jnp.sum(selector * rank_sizes.astype(F32)[None, :], axis=1)
    matches = (token_adapter[:, None] == column_owner[None, :]).astype(F32)
    return matches * (ADAPTER_ALPHA / token_rank)[:, None]


def nn(a, b):
    return jnp.dot(a, b, preferred_element_type=F32)


def nt(a, b):
    return lax.dot_general(a, b, (((1,), (1,)), ((), ())), preferred_element_type=F32)


def tn(a, b):
    return lax.dot_general(a, b, (((0,), (0,)), ((), ())), preferred_element_type=F32)


def kernel(
    S, n, D,
    x_hbm, g_hbm, wv_hbm, wo_hbm, at_hbm, up_hbm, gain_hbm, coef_ref,
    gd_ref, gu_ref,
    xs, gs, wv, wo, wa, up, gain, st, s1in, s2out, s2in, agf, agb, ukeep, ikeep, gbuf, gin, gown,
    loc_sem, xsend, xrecv, osend, orecv, rsend, rrecv, dsend, drecv,
    s1_sem, s2send, s2recv, agsend, agrecv, agp_sem, rlsend, rlrecv, gsend, grecv,
):
    sec = lax.axis_index("section")
    f = lax.axis_index("fsdp")
    h = n // 2
    q = f // 2
    c = f % 2
    partner = q * 2 + 1 - c
    rq, dl = xs.shape[2:]
    T = n * rq
    V = up.shape[2]
    packed = at_hbm.shape[0]
    wide = up.shape[1]
    s1 = sec + 1 - 2 * (sec % 2)
    s2 = (sec + 2) % S
    s3 = (s1 + 2) % S

    def rc(src, dst, ssem, rsem, section, fs):
        return pltpu.make_async_remote_copy(
            src_ref=src, dst_ref=dst, send_sem=ssem, recv_sem=rsem,
            device_id=(section, fs), device_id_type=MESH)

    barrier = pltpu.get_barrier_semaphore()
    for k in range(1, n):
        pl.semaphore_signal(barrier, inc=1, device_id=(sec, (f + k) % n), device_id_type=MESH)
    for k in range(1, S):
        pl.semaphore_signal(barrier, inc=1, device_id=((sec + k) % S, f), device_id_type=MESH)
    for r, fill in ((wa, packed), (up, packed)):
        r[:, fill:, :] = jnp.zeros((S, wide - fill, r.shape[2]), r.dtype)
    pl.semaphore_wait(barrier, n - 1 + S - 1)

    pending = []
    local = []

    def own(i, src, slots, rows):
        half = rows // 2
        cp = pltpu.make_async_copy(src, slots.at[sec, pl.ds(0, rows)], loc_sem.at[i])
        cp.start()
        local.append(cp)
        for d, peer, order in ((0, s1, (0, 1)), (1, s2, (1, 0))):
            for b in order:
                r = rc(src.at[pl.ds(b * half, half)], slots.at[sec, pl.ds(b * half, half)],
                       osend.at[i, d, b], orecv.at[i, d, b], peer, f)
                r.start()
                pending.append(r)

    def got(i, slots, rows, d, b, slot):
        half = rows // 2
        ref = slots.at[slot, pl.ds(b * half, half)]
        rc(ref, ref, osend.at[i, d, b], orecv.at[i, d, b], s1, f).wait_recv()
        return ref

    def relay(i, slots, rows):
        for d, slot, peer in ((0, s1, s2), (1, s2, s1)):
            ref = got(i, slots, rows, d, d, slot)
            r = rc(ref, ref, rsend.at[i, d], rrecv.at[i, d], peer, f)
            r.start()
            pending.append(r)

    def finish(i, slots, rows):
        half = rows // 2
        got(i, slots, rows, 0, 1, s1)
        got(i, slots, rows, 1, 0, s2)
        for d in (0, 1):
            ref = slots.at[s3, pl.ds(d * half, half)]
            rc(ref, ref, rsend.at[i, d], rrecv.at[i, d], s1, f).wait_recv()

    def exchange(i, src, dst):
        mine = src.at[pl.ds(sec * rq, rq)]
        cp = pltpu.make_async_copy(mine.at[:, pl.ds(pl.multiple_of(f * dl, LANES), dl)], dst.at[f], loc_sem.at[3 + i])
        cp.start()
        local.append(cp)
        for k in range(1, n):
            p = (f + k) % n
            r = rc(mine.at[:, pl.ds(pl.multiple_of(p * dl, LANES), dl)], dst.at[f],
                   xsend.at[i, k], xrecv.at[i, k], sec, p)
            r.start()
            pending.append(r)

    def exchanged(i, dst):
        for k in range(1, n):
            ref = dst.at[(f + n - k) % n]
            rc(ref, ref, xsend.at[i, k], xrecv.at[i, k], sec, f).wait_recv()

    half_v, half_o = wv.shape[1], wo.shape[1]
    exchange(0, x_hbm, xs.at[0])
    own(0, wv_hbm, wv, half_v)
    own(1, at_hbm, wa, packed)
    for j, (src, slots, rows) in enumerate(((up_hbm, up, packed), (gain_hbm, gain, gain.shape[1]))):
        cp = pltpu.make_async_copy(src, slots.at[sec, pl.ds(0, rows)], loc_sem.at[5 + j])
        cp.start()
        local.append(cp)
        for k in range(1, S):
            r = rc(src, slots.at[sec, pl.ds(0, rows)], dsend.at[j, k], drecv.at[j, k], (sec + k) % S, f)
            r.start()
            pending.append(r)
    exchange(1, g_hbm, gs)
    relay(0, wv, half_v)
    relay(1, wa, packed)
    own(2, wo_hbm, wo, half_o)
    for cp in local:
        cp.wait()
    exchanged(0, xs.at[0])
    finish(0, wv, half_v)
    finish(1, wa, packed)
    for j, (slots, rows) in enumerate(((up, packed), (gain, gain.shape[1]))):
        for k in range(1, S):
            ref = slots.at[(sec + S - k) % S, pl.ds(0, rows)]
            rc(ref, ref, dsend.at[j, k], drecv.at[j, k], sec, f).wait_recv()

    low_col = lax.broadcasted_iota(jnp.int32, (1, wide), 1)

    def scatter(width, between):
        s1c = rc(st.at[:, 1 - c, :, pl.ds(0, width)], s1in.at[:, :, pl.ds(0, width)],
                 s1_sem.at[0], s1_sem.at[1], sec, partner)
        s1c.start()
        between()
        s1c.wait_recv()
        sends = []
        for k in range(1, h):
            to = (q + k) % h
            s2out[k, :, pl.ds(0, width)] = (
                st[to, c, :, pl.ds(0, width)].astype(F32) + s1in[to, :, pl.ds(0, width)].astype(F32)
            ).astype(BF16)
            r = rc(s2out.at[k, :, pl.ds(0, width)], s2in.at[k, :, pl.ds(0, width)],
                   s2send.at[k], s2recv.at[k], sec, to * 2 + c)
            r.start()
            sends.append(r)
        total = st[q, c, :, pl.ds(0, width)].astype(F32) + s1in[q, :, pl.ds(0, width)].astype(F32)
        for k in range(1, h):
            sends[k - 1].wait_recv()
            total = total + s2in[k, :, pl.ds(0, width)].astype(F32)
        s1c.wait_send()
        for r in sends:
            r.wait_send()
        return total

    def gather(buf):
        mine = buf.at[f]
        sends = []
        for k in range(1, h):
            r = rc(mine, mine, agsend.at[k], agrecv.at[k], sec, ((q + k) % h) * 2 + c)
            r.start()
            sends.append(r)
        r = rc(mine, mine, agp_sem.at[0], agp_sem.at[1], sec, partner)
        r.start()
        sends.append(r)
        for k in range(1, h):
            ref = buf.at[((q + h - k) % h) * 2 + c]
            rc(ref, ref, agsend.at[k], agrecv.at[k], sec, partner).wait_recv()
            r = rc(ref, ref, rlsend.at[k], rlrecv.at[k], sec, partner)
            r.start()
            sends.append(r)
        ref = buf.at[partner]
        rc(ref, ref, agp_sem.at[0], agp_sem.at[1], sec, partner).wait_recv()
        for k in range(1, h):
            ref = buf.at[((q + h - k) % h) * 2 + 1 - c]
            rc(ref, ref, rlsend.at[k], rlrecv.at[k], sec, partner).wait_recv()
        for r in sends:
            r.wait_send()

    def gained(l):
        return (xs[l].reshape(T, dl).astype(F32) * gain[l][0:1, :]).astype(BF16)

    def forward(l, carry):
        x32 = xs[l].reshape(T, dl).astype(F32)
        square = jnp.sum(x32 * x32, axis=1, keepdims=True)
        xg = (x32 * gain[l][0:1, :]).astype(BF16)
        st[:, :, :, 0:V] = nn(xg, wv[l]).astype(BF16).reshape(h, 2, rq, V)
        low = jnp.where(low_col == packed, square, nt(xg, wa[l]))
        st[:, :, :, V:V + wide] = low.astype(BF16).reshape(h, 2, rq, wide)
        total = scatter(V + wide, lambda: None)
        tail = total[:, V:]
        mean = jnp.sum(jnp.where(low_col == packed, tail, 0.0), axis=1, keepdims=True) / D
        inv = lax.rsqrt(mean + EPSILON)
        lowp = tail * coef_ref[...]
        value = total[:, :V] * inv + nn((lowp * inv).astype(BF16), up[l])
        ukeep[l] = total
        ikeep[l] = jnp.broadcast_to(inv, (rq, LANES))
        agf[l, f, :, 0:V] = value.astype(BF16)
        agf[l, f, :, V:V + wide] = lowp.astype(BF16)
        gather(agf.at[l])

        @pl.when(l == 0)
        def _():
            relay(2, wo, half_o)
            finish(2, wo, half_o)

        @pl.when(l < S - 1)
        def _():
            out = nn(agf[l, :, :, 0:V].reshape(T, V), wo[l])
            xs[l + 1] = (xs[l].reshape(T, dl).astype(F32) + out).astype(BF16).reshape(n, rq, dl)

        return carry

    before = len(pending)
    lax.fori_loop(0, S, forward, 0)
    late = pending[before:]
    del pending[before:]
    exchanged(1, gs)

    part = V // n

    def gradients(l):
        slot = l % 2
        hv = agb[slot, :, :, 0:V].reshape(T, V)
        hl = agb[slot, :, :, V:V + wide].reshape(T, wide)
        down = tn(hl, gained(l))[:packed]
        row = lax.broadcasted_iota(jnp.int32, (V, LANES), 0)
        col = lax.broadcasted_iota(jnp.int32, (V, LANES), 1)
        pick = jnp.where((row == col + f * part) & (col < part), 1.0, 0.0).astype(BF16)
        cut = nn(hv, pick).astype(BF16)
        upper = tn(agf[l, :, :, V:V + wide].reshape(T, wide), cut)[:packed]

        @pl.when(sec == l)
        def _():
            gown[:, 0:dl] = down
            gown[:, dl:dl + LANES] = upper

        @pl.when(sec != l)
        def _():
            gbuf[l, :, 0:dl] = down.astype(BF16)
            gbuf[l, :, dl:dl + LANES] = upper.astype(BF16)
            rel = (sec - l + S) % S
            rc(gbuf.at[l], gin.at[rel], gsend.at[l], grecv.at[rel], l, f).start()

    def backward(step, carry):
        l = S - 1 - step
        slot = l % 2
        st[:, :, :, 0:V] = nt(gs[...].reshape(T, dl), wo[l]).astype(BF16).reshape(h, 2, rq, V)

        def between():
            @pl.when(step > 0)
            def _():
                gradients(l + 1)

        vg = scatter(V, between).astype(BF16)
        inv = ikeep[l][:, 0:1]
        lg = (nt(vg, up[l]) * coef_ref[...]).astype(BF16)
        u = ukeep[l]
        vg32, lg32 = vg.astype(F32), lg.astype(F32)
        dot = jnp.sum(vg32 * u[:, :V], axis=1, keepdims=True)
        dot = dot + jnp.sum(lg32 * u[:, V:], axis=1, keepdims=True)
        cc = inv * inv * inv * (dot / D)
        high = cc.astype(BF16).astype(F32)
        rest = cc - high
        agb[slot, f, :, 0:V] = (vg32 * inv).astype(BF16)
        tail = jnp.where(low_col == packed, high, jnp.where(low_col == packed + 1, rest, lg32 * inv))
        agb[slot, f, :, V:V + wide] = tail.astype(BF16)
        gather(agb.at[slot])

        @pl.when(l > 0)
        def _():
            hl = agb[slot, :, :, V:V + wide].reshape(T, wide)
            back = nt(agb[slot, :, :, 0:V].reshape(T, V), wv[l]) + nn(hl, wa[l])
            both = (low_col == packed) | (low_col == packed + 1)
            c_all = jnp.sum(jnp.where(both, hl.astype(F32), 0.0), axis=1, keepdims=True)
            new = gs[...].reshape(T, dl).astype(F32) + back * gain[l][0:1, :]
            new = new - c_all * xs[l].reshape(T, dl).astype(F32)
            gs[...] = new.astype(BF16).reshape(n, rq, dl)

        return carry

    lax.fori_loop(0, S, backward, 0)
    gradients(0)

    total = gown[...]
    for k in range(1, S):
        ref = gin.at[k]
        rc(ref, ref, gsend.at[0], grecv.at[k], sec, f).wait_recv()
        total = total + gin[k].astype(F32)
    gu_ref[...] = total[:, dl:dl + part]
    square = jnp.concatenate([total[:, 0:dl], jnp.zeros((wide - packed, dl), F32)], axis=0)
    gd_ref[...] = square.T[:, :packed]
    for r in pending:
        r.wait_send()
    for l in range(S):
        @pl.when(sec != l)
        def _():
            rc(gbuf.at[l], gin.at[1], gsend.at[l], grecv.at[1], l, f).wait_send()
    half = half_o // 2
    for d, slot, peer in ((0, s1, s2), (1, s2, s1)):
        ref = wo.at[slot, pl.ds(d * half, half)]
        rc(ref, ref, rsend.at[2, d], rrecv.at[2, d], peer, f).wait_send()


def local(
    residual_input,
    output_gradient,
    value_projection_weight,
    output_weight,
    adapter_down_weight,
    adapter_up_weight,
    input_norm_scale,
    segment_adapter_index,
    adapter_rank_blocks,
):
    S = lax.axis_size("section")
    n = lax.axis_size("fsdp")
    sec = lax.axis_index("section")
    f = lax.axis_index("fsdp")
    micro, rows, D = residual_input.shape
    V = value_projection_weight.shape[2]
    packed = adapter_down_weight.shape[2]
    wide = -(-packed // (2 * LANES)) * 2 * LANES
    dl = D // n
    R = micro * rows
    rq = R // S
    h = n // 2
    coef = coefficients(segment_adapter_index.reshape(-1), adapter_rank_blocks, wide)
    coef = lax.dynamic_slice_in_dim(coef, sec * rq, rq, 0)
    at = lax.dynamic_slice_in_dim(adapter_down_weight[0], f * dl, dl, 0).T
    gain = jnp.broadcast_to(lax.dynamic_slice_in_dim(input_norm_scale, f * dl, dl, 1), (8, dl))
    W = V + wide
    any_ = pl.BlockSpec(memory_space=pl.ANY)
    vm = pl.BlockSpec(memory_space=pltpu.VMEM)
    DMA = pltpu.SemaphoreType.DMA
    gd, gu = pl.pallas_call(
        functools.partial(kernel, S, n, D),
        out_shape=(
            jax.ShapeDtypeStruct((dl, packed), F32),
            jax.ShapeDtypeStruct((packed, V // n), F32),
        ),
        in_specs=[any_] * 7 + [vm],
        out_specs=(vm, vm),
        scratch_shapes=[
            pltpu.VMEM((S, n, rq, dl), BF16),
            pltpu.VMEM((n, rq, dl), BF16),
            pltpu.VMEM((S, dl, V), BF16),
            pltpu.VMEM((S, V, dl), BF16),
            pltpu.VMEM((S, wide, dl), BF16),
            pltpu.VMEM((S, wide, V), BF16),
            pltpu.VMEM((S, 8, dl), F32),
            pltpu.VMEM((h, 2, rq, W), BF16),
            pltpu.VMEM((h, rq, W), BF16),
            pltpu.VMEM((h, rq, W), BF16),
            pltpu.VMEM((h, rq, W), BF16),
            pltpu.VMEM((S, n, rq, W), BF16),
            pltpu.VMEM((2, n, rq, W), BF16),
            pltpu.VMEM((S, rq, W), F32),
            pltpu.VMEM((S, rq, LANES), F32),
            pltpu.VMEM((S, packed, dl + LANES), BF16),
            pltpu.VMEM((S, packed, dl + LANES), BF16),
            pltpu.VMEM((packed, dl + LANES), F32),
            DMA((7,)), DMA((2, n)), DMA((2, n)),
            DMA((3, 2, 2)), DMA((3, 2, 2)), DMA((3, 2)), DMA((3, 2)),
            DMA((2, S)), DMA((2, S)),
            DMA((2,)), DMA((h,)), DMA((h,)),
            DMA((h,)), DMA((h,)), DMA((2,)), DMA((h,)), DMA((h,)),
            DMA((S,)), DMA((S,)),
        ],
        compiler_params=pltpu.CompilerParams(
            collective_id=0, has_side_effects=True, vmem_limit_bytes=60 * 1024 * 1024
        ),
    )(
        residual_input.reshape(R, D), output_gradient.reshape(R, D),
        value_projection_weight[0], output_weight[0], at, adapter_up_weight[0], gain, coef,
    )
    return (gd[None], gu[None])


def solution(mesh):
    placed = (
        P(None, "fsdp", None),
        P(None, "fsdp", None),
        P("section", "fsdp", None),
        P("section", None, "fsdp"),
        P("section", None, None),
        P("section", None, None),
        P("section", None),
        P(None, "fsdp"),
        P(),
    )
    return jax.shard_map(
        local,
        mesh=mesh,
        in_specs=placed,
        out_specs=(P("section", "fsdp", None), P("section", None, "fsdp")),
        check_vma=False,
    )
```

```python
import functools

import jax
import jax.numpy as jnp
from jax import lax
from jax.experimental import pallas as pl
from jax.experimental.pallas import tpu as pltpu
from jax.sharding import PartitionSpec as P

SEG = 32
EPSILON = 1e-06
ADAPTER_ALPHA = 32.0
LANES = 128
MESH = pl.DeviceIdType.MESH
F32 = jnp.float32
BF16 = jnp.bfloat16


def nn(a, b):
    return jnp.dot(a, b, preferred_element_type=F32)


def nt(a, b):
    return lax.dot_general(a, b, (((1,), (1,)), ((), ())), preferred_element_type=F32)


def tn(a, b):
    return lax.dot_general(a, b, (((0,), (0,)), ((), ())), preferred_element_type=F32)


def kernel(
    S, n, D,
    x_hbm, g_hbm, wv_hbm, wo_hbm, at_hbm, up_hbm, gain_hbm, seg_ref, rank_ref,
    gd_ref, gu_ref,
    xs, gs, wv, wo, wa, up, gain, st, s1in, s2out, s2in, agf, agb, ukeep, ikeep, gbuf, gin, gown, coef_ref,
    loc_sem, xsend, xrecv, osend, orecv, rsend, rrecv, dsend, drecv,
    s1_sem, s2send, s2recv, agsend, agrecv, agp_sem, rlsend, rlrecv, gsend, grecv,
):
    sec = lax.axis_index("section")
    f = lax.axis_index("fsdp")
    h = n // 2
    q = f // 2
    c = f % 2
    partner = q * 2 + 1 - c
    rq, dl = xs.shape[2:]
    T = n * rq
    V = up.shape[2]
    packed = at_hbm.shape[0]
    wide = up.shape[1]
    s1 = sec + 1 - 2 * (sec % 2)
    s2 = (sec + 2) % S
    s3 = (s1 + 2) % S

    def rc(src, dst, ssem, rsem, section, fs):
        return pltpu.make_async_remote_copy(
            src_ref=src, dst_ref=dst, send_sem=ssem, recv_sem=rsem,
            device_id=(section, fs), device_id_type=MESH)

    adapters = rank_ref.shape[0]
    per = seg_ref.shape[1]
    column = lax.broadcasted_iota(jnp.int32, (SEG, wide), 1)
    for j in range(rq // SEG):
        spot = sec * (rq // SEG) + j
        mine = seg_ref[spot // per, spot % per]
        begin, size = jnp.int32(0), jnp.int32(0)
        for a in range(adapters):
            rank = 8 * rank_ref[a]
            begin = begin + jnp.where(mine > a, rank, 0)
            size = size + jnp.where(mine == a, rank, 0)
        inside = (column >= begin) & (column < begin + size)
        scale = ADAPTER_ALPHA / jnp.full((SEG, wide), size, jnp.int32).astype(F32)
        coef_ref[j * SEG:(j + 1) * SEG, :] = jnp.where(inside, scale, 0.0)

    barrier = pltpu.get_barrier_semaphore()
    for k in range(1, n):
        pl.semaphore_signal(barrier, inc=1, device_id=(sec, (f + k) % n), device_id_type=MESH)
    for k in range(1, S):
        pl.semaphore_signal(barrier, inc=1, device_id=((sec + k) % S, f), device_id_type=MESH)
    for r, fill in ((wa, packed), (up, packed)):
        r[:, fill:, :] = jnp.zeros((S, wide - fill, r.shape[2]), r.dtype)
    pl.semaphore_wait(barrier, n - 1 + S - 1)

    pending = []
    local = []

    arrays = (
        (wv_hbm, wv, wv.shape[1]), (at_hbm, wa, packed), (wo_hbm, wo, wo.shape[1]), (up_hbm, up, packed)
    )
    peers = (s1, s2)

    def piece(i, d, b):
        src, slots, rows = arrays[i]
        half = rows // 2
        return rc(src.at[pl.ds(b * half, half)], slots.at[sec, pl.ds(b * half, half)],
                  osend.at[i, d, b], orecv.at[i, d, b], peers[d], f)

    def passed(i, d):
        _, slots, rows = arrays[i]
        half = rows // 2
        ref = slots.at[peers[d], pl.ds(d * half, half)]
        return rc(ref, ref, rsend.at[i, d], rrecv.at[i, d], peers[1 - d], f)

    def keep(i):
        src, slots, rows = arrays[i]
        cp = pltpu.make_async_copy(src, slots.at[sec, pl.ds(0, rows)], loc_sem.at[i])
        cp.start()
        local.append(cp)

    def first(i):
        for d in (0, 1):
            piece(i, d, d).start()

    def second(i):
        for d in (0, 1):
            piece(i, d, 1 - d).start()

    def got(i, d, b):
        _, slots, rows = arrays[i]
        half = rows // 2
        ref = slots.at[peers[d], pl.ds(b * half, half)]
        rc(ref, ref, osend.at[i, d, b], orecv.at[i, d, b], peers[d], f).wait_recv()

    def relay(i):
        for d in (0, 1):
            got(i, d, d)
            passed(i, d).start()

    def arrive(i, l):
        _, slots, rows = arrays[i]
        half = rows // 2
        for d in (0, 1):
            @pl.when(l == peers[d])
            def _():
                got(i, d, 1 - d)

        @pl.when(l == s3)
        def _():
            for d in (0, 1):
                ref = slots.at[s3, pl.ds(d * half, half)]
                rc(ref, ref, rsend.at[i, d], rrecv.at[i, d], s1, f).wait_recv()

    def exchange(i, src, dst):
        mine = src.at[pl.ds(sec * rq, rq)]
        cp = pltpu.make_async_copy(mine.at[:, pl.ds(pl.multiple_of(f * dl, LANES), dl)], dst.at[f], loc_sem.at[4 + i])
        cp.start()
        local.append(cp)
        for k in range(1, n):
            p = (f + k) % n
            r = rc(mine.at[:, pl.ds(pl.multiple_of(p * dl, LANES), dl)], dst.at[f],
                   xsend.at[i, k], xrecv.at[i, k], sec, p)
            r.start()
            pending.append(r)

    def exchanged(i, dst):
        for k in range(1, n):
            ref = dst.at[(f + n - k) % n]
            rc(ref, ref, xsend.at[i, k], xrecv.at[i, k], sec, f).wait_recv()

    outer = (sec == 0) | (sec == S - 1)
    exchange(0, x_hbm, xs.at[0])
    for i in (0, 1, 3):
        first(i)

    @pl.when(outer)
    def _():
        for i in (0, 1, 3):
            second(i)
        first(2)
        second(2)

    for i in range(4):
        keep(i)
    cp = pltpu.make_async_copy(gain_hbm, gain.at[sec], loc_sem.at[6])
    cp.start()
    local.append(cp)
    for k in range(1, S):
        r = rc(gain_hbm, gain.at[sec], dsend.at[k], drecv.at[k], (sec + k) % S, f)
        r.start()
        pending.append(r)
    exchange(1, g_hbm, gs)
    for i in (0, 1, 3):
        relay(i)

    @pl.when(jnp.logical_not(outer))
    def _():
        for i in (0, 1, 3):
            second(i)
        relay(2)
        first(2)
        second(2)

    for cp in local:
        cp.wait()
    exchanged(0, xs.at[0])
    for k in range(1, S):
        ref = gain.at[(sec + S - k) % S]
        rc(ref, ref, dsend.at[k], drecv.at[k], sec, f).wait_recv()

    low_col = lax.broadcasted_iota(jnp.int32, (1, wide), 1)

    def scatter(width, t, early, between):
        s1c = rc(st.at[:, 1 - c, :, pl.ds(0, width)], s1in.at[t, :, :, pl.ds(0, width)],
                 s1_sem.at[t, 0], s1_sem.at[t, 1], sec, partner)
        s1c.start()
        early()
        s1c.wait_recv()
        sends = []
        for k in range(1, h):
            to = (q + k) % h
            s2out[k, :, pl.ds(0, width)] = (
                st[to, c, :, pl.ds(0, width)].astype(F32) + s1in[t, to, :, pl.ds(0, width)].astype(F32)
            ).astype(BF16)
            r = rc(s2out.at[k, :, pl.ds(0, width)], s2in.at[t, k, :, pl.ds(0, width)],
                   s2send.at[t, k], s2recv.at[t, k], sec, to * 2 + c)
            r.start()
            sends.append(r)
        between()
        total = st[q, c, :, pl.ds(0, width)].astype(F32) + s1in[t, q, :, pl.ds(0, width)].astype(F32)
        for k in range(1, h):
            sends[k - 1].wait_recv()
            total = total + s2in[t, k, :, pl.ds(0, width)].astype(F32)
        s1c.wait_send()
        for r in sends:
            r.wait_send()
        return total

    def gather(buf, t):
        mine = buf.at[f]
        sends = []
        for k in range(1, h):
            r = rc(mine, mine, agsend.at[t, k], agrecv.at[t, k], sec, ((q + k) % h) * 2 + c)
            r.start()
            sends.append(r)
        r = rc(mine, mine, agp_sem.at[t, 0], agp_sem.at[t, 1], sec, partner)
        r.start()
        sends.append(r)
        for k in range(1, h):
            ref = buf.at[((q + h - k) % h) * 2 + c]
            rc(ref, ref, agsend.at[t, k], agrecv.at[t, k], sec, partner).wait_recv()
            r = rc(ref, ref, rlsend.at[t, k], rlrecv.at[t, k], sec, partner)
            r.start()
            sends.append(r)
        ref = buf.at[partner]
        rc(ref, ref, agp_sem.at[t, 0], agp_sem.at[t, 1], sec, partner).wait_recv()
        for k in range(1, h):
            ref = buf.at[((q + h - k) % h) * 2 + 1 - c]
            rc(ref, ref, rlsend.at[t, k], rlrecv.at[t, k], sec, partner).wait_recv()
        for r in sends:
            r.wait_send()

    def gained(l):
        return (xs[l].reshape(T, dl).astype(F32) * gain[l][0:1, :]).astype(BF16)

    def forward(l, carry):
        for i in (0, 1, 3):
            arrive(i, l)
        x32 = xs[l].reshape(T, dl).astype(F32)
        square = jnp.sum(x32 * x32, axis=1, keepdims=True)
        xg = (x32 * gain[l][0:1, :]).astype(BF16)
        st[:, :, :, 0:V] = nn(xg, wv[l]).astype(BF16).reshape(h, 2, rq, V)
        low = jnp.where(low_col == packed, square, nt(xg, wa[l]))
        st[:, :, :, V:V + wide] = low.astype(BF16).reshape(h, 2, rq, wide)
        total = scatter(V + wide, 0, lambda: None, lambda: None)
        tail = total[:, V:]
        mean = jnp.sum(jnp.where(low_col == packed, tail, 0.0), axis=1, keepdims=True) / D
        inv = lax.rsqrt(mean + EPSILON)
        lowp = tail * coef_ref[...]
        value = total[:, :V] * inv + nn((lowp * inv).astype(BF16), up[l])
        ukeep[l] = total
        ikeep[l] = jnp.broadcast_to(inv, (rq, LANES))
        agf[l, f, :, 0:V] = value.astype(BF16)
        agf[l, f, :, V:V + wide] = lowp.astype(BF16)

        @pl.when(l < S - 1)
        def _():
            gather(agf.at[l], 0)

        @pl.when((l == 0) & outer)
        def _():
            relay(2)

        arrive(2, l)

        @pl.when(l < S - 1)
        def _():
            out = nn(agf[l, :, :, 0:V].reshape(T, V), wo[l])
            xs[l + 1] = (xs[l].reshape(T, dl).astype(F32) + out).astype(BF16).reshape(n, rq, dl)

        return carry

    lax.fori_loop(0, S, forward, 0)
    exchanged(1, gs)

    part = V // n

    def gradients(l):
        slot = l % 2
        hv = agb[slot, :, :, 0:V].reshape(T, V)
        hl = agb[slot, :, :, V:V + wide].reshape(T, wide)
        down = tn(hl, gained(l))[:packed]
        row = lax.broadcasted_iota(jnp.int32, (V, LANES), 0)
        col = lax.broadcasted_iota(jnp.int32, (V, LANES), 1)
        pick = jnp.where((row == col + f * part) & (col < part), 1.0, 0.0).astype(BF16)
        cut = nn(hv, pick).astype(BF16)
        upper = tn(agf[l, :, :, V:V + wide].reshape(T, wide), cut)[:packed]

        @pl.when(sec == l)
        def _():
            gown[:, 0:dl] = down
            gown[:, dl:dl + LANES] = upper

        @pl.when(sec != l)
        def _():
            gbuf[l, :, 0:dl] = down.astype(BF16)
            gbuf[l, :, dl:dl + LANES] = upper.astype(BF16)
            rel = (sec - l + S) % S
            rc(gbuf.at[l], gin.at[rel], gsend.at[l], grecv.at[rel], l, f).start()

    def backward(step, carry):
        l = S - 1 - step
        slot = l % 2
        st[:, :, :, 0:V] = nt(gs[...].reshape(T, dl), wo[l]).astype(BF16).reshape(h, 2, rq, V)

        def between():
            @pl.when(step == 0)
            def _():
                gather(agf.at[S - 1], 1)

            @pl.when(step > 0)
            def _():
                gradients(l + 1)

        vg = scatter(V, 1, lambda: None, between).astype(BF16)
        inv = ikeep[l][:, 0:1]
        lg = (nt(vg, up[l]) * coef_ref[...]).astype(BF16)
        u = ukeep[l]
        vg32, lg32 = vg.astype(F32), lg.astype(F32)
        dot = jnp.sum(vg32 * u[:, :V], axis=1, keepdims=True)
        dot = dot + jnp.sum(lg32 * u[:, V:], axis=1, keepdims=True)
        cc = inv * inv * inv * (dot / D)
        high = cc.astype(BF16).astype(F32)
        rest = cc - high
        agb[slot, f, :, 0:V] = (vg32 * inv).astype(BF16)
        tail = jnp.where(low_col == packed, high, jnp.where(low_col == packed + 1, rest, lg32 * inv))
        agb[slot, f, :, V:V + wide] = tail.astype(BF16)
        gather(agb.at[slot], 0)

        @pl.when(l > 0)
        def _():
            hl = agb[slot, :, :, V:V + wide].reshape(T, wide)
            back = nt(agb[slot, :, :, 0:V].reshape(T, V), wv[l]) + nn(hl, wa[l])
            both = (low_col == packed) | (low_col == packed + 1)
            c_all = jnp.sum(jnp.where(both, hl.astype(F32), 0.0), axis=1, keepdims=True)
            new = gs[...].reshape(T, dl).astype(F32) + back * gain[l][0:1, :]
            new = new - c_all * xs[l].reshape(T, dl).astype(F32)
            gs[...] = new.astype(BF16).reshape(n, rq, dl)

        return carry

    lax.fori_loop(0, S, backward, 0)
    gradients(0)

    total = gown[...]
    for k in range(1, S):
        ref = gin.at[k]
        rc(ref, ref, gsend.at[0], grecv.at[k], sec, f).wait_recv()
        total = total + gin[k].astype(F32)
    gu_ref[...] = total[:, dl:dl + part]
    square = jnp.concatenate([total[:, 0:dl], jnp.zeros((wide - packed, dl), F32)], axis=0)
    gd_ref[...] = square.T[:, :packed]
    for r in pending:
        r.wait_send()
    for l in range(S):
        @pl.when(sec != l)
        def _():
            rc(gbuf.at[l], gin.at[1], gsend.at[l], grecv.at[1], l, f).wait_send()
    for i in range(4):
        for d in (0, 1):
            piece(i, d, 0).wait_send()
            piece(i, d, 1).wait_send()
            passed(i, d).wait_send()


def local(
    residual_input,
    output_gradient,
    value_projection_weight,
    output_weight,
    adapter_down_weight,
    adapter_up_weight,
    input_norm_scale,
    segment_adapter_index,
    adapter_rank_blocks,
):
    S = lax.axis_size("section")
    n = lax.axis_size("fsdp")
    f = lax.axis_index("fsdp")
    micro, rows, D = residual_input.shape
    V = value_projection_weight.shape[2]
    packed = adapter_down_weight.shape[2]
    wide = -(-packed // (2 * LANES)) * 2 * LANES
    dl = D // n
    R = micro * rows
    rq = R // S
    h = n // 2
    at = lax.dynamic_slice_in_dim(adapter_down_weight[0], f * dl, dl, 0).T
    gain = jnp.broadcast_to(lax.dynamic_slice_in_dim(input_norm_scale, f * dl, dl, 1), (8, dl))
    W = V + wide
    any_ = pl.BlockSpec(memory_space=pl.ANY)
    vm = pl.BlockSpec(memory_space=pltpu.VMEM)
    sm = pl.BlockSpec(memory_space=pltpu.SMEM)
    DMA = pltpu.SemaphoreType.DMA
    gd, gu = pl.pallas_call(
        functools.partial(kernel, S, n, D),
        out_shape=(
            jax.ShapeDtypeStruct((dl, packed), F32),
            jax.ShapeDtypeStruct((packed, V // n), F32),
        ),
        in_specs=[any_] * 7 + [sm, sm],
        out_specs=(vm, vm),
        scratch_shapes=[
            pltpu.VMEM((S, n, rq, dl), BF16),
            pltpu.VMEM((n, rq, dl), BF16),
            pltpu.VMEM((S, dl, V), BF16),
            pltpu.VMEM((S, V, dl), BF16),
            pltpu.VMEM((S, wide, dl), BF16),
            pltpu.VMEM((S, wide, V), BF16),
            pltpu.VMEM((S, 8, dl), F32),
            pltpu.VMEM((h, 2, rq, W), BF16),
            pltpu.VMEM((2, h, rq, W), BF16),
            pltpu.VMEM((h, rq, W), BF16),
            pltpu.VMEM((2, h, rq, W), BF16),
            pltpu.VMEM((S, n, rq, W), BF16),
            pltpu.VMEM((2, n, rq, W), BF16),
            pltpu.VMEM((S, rq, W), F32),
            pltpu.VMEM((S, rq, LANES), F32),
            pltpu.VMEM((S, packed, dl + LANES), BF16),
            pltpu.VMEM((S, packed, dl + LANES), BF16),
            pltpu.VMEM((packed, dl + LANES), F32),
            pltpu.VMEM((rq, wide), F32),
            DMA((7,)), DMA((2, n)), DMA((2, n)),
            DMA((4, 2, 2)), DMA((4, 2, 2)), DMA((4, 2)), DMA((4, 2)),
            DMA((S,)), DMA((S,)),
            DMA((2, 2)), DMA((2, h)), DMA((2, h)),
            DMA((2, h)), DMA((2, h)), DMA((2, 2)), DMA((2, h)), DMA((2, h)),
            DMA((S,)), DMA((S,)),
        ],
        compiler_params=pltpu.CompilerParams(
            collective_id=0, has_side_effects=True, vmem_limit_bytes=60 * 1024 * 1024
        ),
    )(
        residual_input.reshape(R, D), output_gradient.reshape(R, D),
        value_projection_weight[0], output_weight[0], at, adapter_up_weight[0], gain,
        segment_adapter_index, adapter_rank_blocks,
    )
    return (gd[None], gu[None])


def solution(mesh):
    placed = (
        P(None, "fsdp", None),
        P(None, "fsdp", None),
        P("section", "fsdp", None),
        P("section", None, "fsdp"),
        P("section", None, None),
        P("section", None, None),
        P("section", None),
        P(None, "fsdp"),
        P(),
    )
    return jax.shard_map(
        local,
        mesh=mesh,
        in_specs=placed,
        out_specs=(P("section", "fsdp", None), P("section", None, "fsdp")),
        check_vma=False,
    )
```
